32 devices in a mesh: dp: 8 (over z, y), tensor: 4 (over x, core).
Axes of the slice: x: 2, y: 2, z: 4, core: 2. Of those that a mesh axis runs over, the one named last changes fastest.
Arguments:
- tree_ids: int32 [8, 64], P('dp'), may hold values from 0 to 65535, as said below
- ancestors: int32 [8, 64, 64], P('dp'), may hold values from 0 to 1, as said below
- lengths: int32 [8], P('dp'), may hold values from 64 to 1024, as said below
- table: bfloat16 [65536, 4096], P('dp', 'tensor'), may hold values from -3 to 3
- gain: bfloat16 [4096], replicated, may hold values from 0.25 to 1.75
- w_query: bfloat16 [4096, 4096], P(None, 'tensor'), may hold values from -0.09375 to 0.09375
- w_kv: bfloat16 [2, 4096, 1024], P(None, None, 'tensor'), may hold values from -0.09375 to 0.09375
- w_out: bfloat16 [4096, 4096], P('tensor'), may hold values from -0.09375 to 0.09375
- key_cache: bfloat16 [8, 8, 1024, 128], P('dp', 'tensor'), may hold values from -480 to 480
- value_cache: bfloat16 [8, 8, 1024, 128], P('dp', 'tensor'), may hold values from -6 to 6
Outputs:
- layer_output: bfloat16 [512, 4096], P('dp', 'tensor')
The draws below stay inside these ranges and needn't reach their ends.
Inputs may be any that keep to these rules, and one draw needn't show every extreme that they name: `tree_ids`: split the vocabulary into equal consecutive parts, one for each index of dp; of the nodes of the rows of one index of dp, at most 16 have ids in any one part, and exactly 16 in some part. Row n of each row's matrix marks node n and all its ancestors in that row's tree; node 0 is the root and every other node's parent has a smaller index. `lengths`: some row has all 1024 slots live.
All inputs are finite; a program needn't handle non-finite values.
Results may differ from the reference program's by a relative error of at most 0.004.
The reference program's roundings to bfloat16 on the way count: a program that leaves them out, or rounds other values in their place, can miss the bound.
Values may be sent and summed in bfloat16 or wider, within the bound.
A program may use at most 128 MiB of HBM per device.

```python
import math
import jax
import jax.numpy as jnp
from jax import lax

D = 4096
HEADS = 32
KVH = 8
HD = 128
VOCAB = 65536
NODES = 64
CTX = 1024
R_DEV = 1
ROWS = 8
TOKENS = 512
CAP = 16
N_DP = 8


def draw_tree_ids(key, part):
    block_size = R_DEV * NODES
    part_rows = VOCAB // N_DP
    block_keys = jax.random.split(key, N_DP)

    def one_block(block_key):
        chosen_key, order_key, place_key, entry_key = jax.random.split(block_key, 4)
        chosen = jax.random.randint(chosen_key, (), 0, N_DP)
        others_index = jnp.arange(CAP * (N_DP - 1), dtype=jnp.int32) // CAP
        others_owner = others_index + (others_index >= chosen).astype(jnp.int32)
        others_owner = jax.random.permutation(order_key, others_owner)
        owners_all = jnp.concatenate([jnp.full((CAP,), chosen, jnp.int32), others_owner])
        owners_block = jax.random.permutation(place_key, owners_all[:block_size])
        entries = jax.random.randint(entry_key, (block_size,), 0, part_rows)
        return (owners_block * part_rows + entries).astype(jnp.int32)
    drawn = jax.vmap(one_block)(block_keys)
    return drawn.reshape(ROWS, NODES).astype(jnp.int32)


def draw_ancestors(key, part):
    raw_bits = jax.random.randint(key, (ROWS, NODES), 0, 2 ** 30)
    node_index = jnp.arange(NODES, dtype=jnp.int32)
    parents = raw_bits % jnp.maximum(node_index, 1)[None, :]

    def build(parent_row):
        start_matrix = jnp.zeros((NODES, NODES), jnp.int32).at[0, 0].set(1)

        def add_node(node, matrix):
            new_row = matrix[parent_row[node]].at[node].set(1)
            return matrix.at[node].set(new_row)
        return lax.fori_loop(1, NODES, add_node, start_matrix)
    return jax.vmap(build)(parents).astype(jnp.int32)


def draw_lengths(key, part):
    first_key, second_key = jax.random.split(key)
    values_drawn = jax.random.randint(first_key, (ROWS,), CTX // 16, CTX + 1)
    chosen = jax.random.randint(second_key, (), 0, ROWS)
    return jnp.where(jnp.arange(ROWS) == chosen, CTX, values_drawn).astype(jnp.int32)


def draw_key_cache(key, part):
    base_draw = jnp.clip(jax.random.normal(key, (ROWS, KVH, CTX, HD), jnp.float32), -8.0, 8.0) * 2.5
    return base_draw.astype(jnp.bfloat16)


def levels(stream_key, shape, cuts, smallest, high):
    level, own = 1.0, jax.random.fold_in(stream_key, 6)
    for position, parts in cuts:
        heights = jnp.exp(jax.random.uniform(jax.random.fold_in(own, position), (parts,), jnp.float32, smallest / len(cuts), high / len(cuts)))
        level = level * jnp.repeat(heights, shape[position] // parts).reshape([-1 if axis == position else 1 for axis in range(len(shape))])
    return level


def normal_values(key, extent, scale, limit, cuts=(), held_as=jnp.bfloat16):
    level = levels(key, extent, cuts, -0.22, 0.18) if cuts else 1.0
    array = jax.random.normal(key, extent, jnp.float32) * scale * level
    return jnp.minimum(jnp.maximum(array, -limit), limit).astype(held_as)


def setup_inputs(seed: int = 0) -> dict:
    seeds = jax.random.split(jax.random.key(seed), 11)
    return {
        "tree_ids": draw_tree_ids(jax.random.fold_in(seeds[10], 71), 0),
        "ancestors": draw_ancestors(jax.random.fold_in(seeds[10], 71), 0),
        "lengths": draw_lengths(jax.random.fold_in(seeds[10], 71), 0),
        "table": normal_values(seeds[3], (VOCAB, D), 0.5, 3.0, ((0, 8), (1, 4))),
        "gain": jnp.clip(1.0 + 0.15 * jax.random.normal(seeds[4], (D,), jnp.float32), 0.25, 1.75).astype(jnp.bfloat16),
        "w_query": normal_values(seeds[5], (D, HEADS * HD), D ** -0.5, 0.09375, ((1, 4),)),
        "w_kv": normal_values(seeds[6], (2, D, KVH * HD), D ** -0.5, 0.09375, ((2, 4),)),
        "w_out": normal_values(seeds[7], (HEADS * HD, D), (HEADS * HD) ** -0.5, 0.09375, ((0, 4),)),
        "key_cache": draw_key_cache(jax.random.fold_in(seeds[10], 71), 0),
        "value_cache": normal_values(seeds[9], (ROWS, KVH, CTX, HD), 1.0, 6.0, ((0, 8), (1, 4))),
    }


EPS = 1e-05
NEG = -1e+30
THETA = 500000.0

def rotary(values, positions):
    half_dim = values.shape[-1] // 2
    freq_index = jnp.arange(half_dim, dtype=jnp.float32)
    inverse = jnp.exp(freq_index * (-2.0 * math.log(THETA) / values.shape[-1]))
    angles = positions[:, None] * inverse[None, :]
    cosine = jnp.cos(angles)[:, None, :]
    sine_part = jnp.sin(angles)[:, None, :]
    lower_half = values[..., :half_dim]
    upper_half = values[..., half_dim:]
    return jnp.concatenate([lower_half * cosine - upper_half * sine_part, upper_half * cosine + lower_half * sine_part], axis=-1)

def contract(left_side, right_side):
    return lax.dot_general(left_side, right_side, (((1,), (1,)), ((), ())), preferred_element_type=jnp.float32)

def attend(query_group, keys_tree, values_tree, keys_cache, values_cache, live_len, tree_mask):
    score_scale = keys_cache.shape[-1] ** (-0.5)
    cache_scores = contract(query_group, keys_cache) * score_scale
    columns = jnp.arange(keys_cache.shape[0], dtype=jnp.int32)
    cache_scores = jnp.where(columns[None, :] < live_len, cache_scores, NEG)
    tree_scores = contract(query_group, keys_tree) * score_scale
    groups = query_group.shape[0] // tree_mask.shape[0]
    tree_scores = jnp.where(jnp.tile(tree_mask, (groups, 1)) > 0, tree_scores, NEG)
    row_top = jnp.maximum(lax.optimization_barrier(jnp.max(cache_scores, axis=1)), lax.optimization_barrier(jnp.max(tree_scores, axis=1)))[:, None]
    cache_exp = jnp.exp(cache_scores - row_top)
    tree_exp = jnp.exp(tree_scores - row_top)
    denominator = lax.optimization_barrier(jnp.sum(cache_exp, axis=1)) + lax.optimization_barrier(jnp.sum(tree_exp, axis=1))
    weighted = jnp.dot(cache_exp.astype(jnp.bfloat16), values_cache, preferred_element_type=jnp.float32)
    weighted = weighted + jnp.dot(tree_exp.astype(jnp.bfloat16), values_tree, preferred_element_type=jnp.float32)
    return (weighted / denominator[:, None]).astype(jnp.bfloat16)

def to_groups(tensor_in, kv_heads, head_dim):
    row_count, node_count, width_all = tensor_in.shape
    per_group = width_all // (kv_heads * head_dim)
    grouped = tensor_in.reshape(row_count, node_count, kv_heads, per_group, head_dim).transpose(0, 2, 3, 1, 4)
    return grouped.reshape(row_count, kv_heads, per_group * node_count, head_dim)

def from_groups(tensor_in, node_count):
    row_count, kv_heads, group_rows, head_dim = tensor_in.shape
    grouped = tensor_in.reshape(row_count, kv_heads, group_rows // node_count, node_count, head_dim)
    return grouped.transpose(0, 3, 1, 2, 4).reshape(row_count, node_count, -1)

def reference(tree_ids, ancestors, lengths, table, gain, w_query, w_kv, w_out, key_cache, value_cache):
    embedded = table[tree_ids.reshape(-1)]
    features = embedded.astype(jnp.float32)
    inv_rms = lax.rsqrt(lax.optimization_barrier(jnp.sum(features * features, axis=1)) / D + EPS)
    normed = (features * inv_rms[:, None] * gain.astype(jnp.float32)[None, :]).astype(jnp.bfloat16)
    queries = jnp.dot(normed, w_query, preferred_element_type=jnp.float32)
    keys_new = jnp.dot(normed, w_kv[0], preferred_element_type=jnp.float32)
    values_new = jnp.dot(normed, w_kv[1], preferred_element_type=jnp.float32).astype(jnp.bfloat16)
    node_depth = lax.optimization_barrier(jnp.sum(ancestors, axis=2)) - 1
    positions = (lengths[:, None] + node_depth).reshape(-1).astype(jnp.float32)
    queries = rotary(queries.reshape(TOKENS, HEADS, HD), positions).astype(jnp.bfloat16).reshape(ROWS, NODES, HEADS * HD)
    keys_new = rotary(keys_new.reshape(TOKENS, KVH, HD), positions).astype(jnp.bfloat16).reshape(ROWS, NODES, KVH * HD)
    values_new = values_new.reshape(ROWS, NODES, KVH * HD)
    query_groups = to_groups(queries, KVH, HD)
    key_groups = to_groups(keys_new, KVH, HD)
    value_groups = to_groups(values_new, KVH, HD)

    def per_row(row_items):
        row_q, row_k, row_v, row_kc, row_vc, live_len, tree_mask = row_items

        def per_head(head_items):
            return attend(head_items[0], head_items[1], head_items[2], head_items[3], head_items[4], live_len, tree_mask)
        return lax.map(per_head, (row_q, row_k, row_v, row_kc, row_vc))
    contexts = lax.map(per_row, (query_groups, key_groups, value_groups, key_cache, value_cache, lengths, ancestors))
    contexts = from_groups(contexts, NODES).reshape(TOKENS, HEADS * HD)
    attention = jnp.dot(contexts, w_out, preferred_element_type=jnp.float32)
    return (features + attention).astype(jnp.bfloat16)
```

```python
import functools
import math

import jax
import jax.numpy as jnp
from jax import lax
from jax.experimental import pallas as pl
from jax.experimental.pallas import tpu as pltpu
from jax.sharding import PartitionSpec as P

EPS = 1e-05
NEG = -1e30
THETA = 500000.0
MESH = pl.DeviceIdType.MESH
LANES = 128


def layer_kernel(
    n_dp,
    n_t,
    nodes,
    capacity,
    ids_ref,
    anc_ref,
    live_ref,
    cos_ref,
    sin_ref,
    gain_ref,
    table_hbm,
    wq_hbm,
    wkv_hbm,
    wout_hbm,
    kc_hbm,
    vc_hbm,
    out_ref,
    ids_all,
    table_v,
    wq_v,
    wkv_v,
    wout_v,
    kc_v,
    vc_v,
    acc,
    slot_send,
    slot_recv,
    emb_all,
    ctx_v,
    rs1_send,
    rs1_recv,
    rs2_send,
    rs2_recv,
    table_sem,
    w_sem,
    wout_sem,
    ids_ssem,
    ids_rsem,
    row_ssem,
    row_rsem,
    own_sem,
    ag_ssem,
    ag_rsem,
    fw_ssem,
    rs1_ssem,
    rs1_rsem,
    rs2_ssem,
    rs2_rsem,
):
    me = lax.axis_index("dp")
    t = lax.axis_index("tensor")
    chip = t // 2
    parity = t % 2
    partner = t + 1 - 2 * parity
    n_chip = n_t // 2
    vocab_rows, width = table_v.shape
    head_dim = kc_v.shape[-1]
    kv_local = kc_v.shape[0]
    heads = wq_v.shape[1] // head_dim
    groups = heads // kv_local
    slots = n_dp * capacity

    n_tab = table_sem.shape[0]
    tab_step = vocab_rows // n_tab
    table_copies = [
        pltpu.make_async_copy(
            table_hbm.at[pl.ds(i * tab_step, tab_step)],
            table_v.at[pl.ds(i * tab_step, tab_step)],
            table_sem.at[i],
        )
        for i in range(n_tab)
    ]
    for copy in table_copies:
        copy.start()

    barrier = pltpu.get_barrier_semaphore()
    for k in range(1, n_dp):
        pl.semaphore_signal(
            barrier, inc=1, device_id={"dp": lax.rem(me + k, n_dp)}, device_id_type=MESH
        )
    for k in range(1, n_t):
        pl.semaphore_signal(
            barrier, inc=1, device_id={"tensor": lax.rem(t + k, n_t)}, device_id_type=MESH
        )
    pl.semaphore_wait(barrier, n_dp + n_t - 2)

    def dp_copy(src, dst, ssem, rsem, k):
        return pltpu.make_async_remote_copy(
            src_ref=src,
            dst_ref=dst,
            send_sem=ssem,
            recv_sem=rsem,
            device_id={"dp": lax.rem(me + k, n_dp)},
            device_id_type=MESH,
        )

    def t_copy(src, dst, ssem, rsem, target):
        return pltpu.make_async_remote_copy(
            src_ref=src,
            dst_ref=dst,
            send_sem=ssem,
            recv_sem=rsem,
            device_id={"tensor": target},
            device_id_type=MESH,
        )

    ids_copies = [
        dp_copy(ids_ref, ids_all.at[k], ids_ssem.at[k], ids_rsem.at[k], k)
        for k in range(1, n_dp)
    ]
    for copy in ids_copies:
        copy.start()

    sub = lax.broadcasted_iota(jnp.int32, (LANES, LANES), 0)
    lane = lax.broadcasted_iota(jnp.int32, (LANES, LANES), 1)
    earlier = (sub < lane).astype(jnp.float32).astype(jnp.bfloat16)
    slot_index = lax.broadcasted_iota(jnp.int32, (slots, LANES), 0)
    slot_block = slot_index // capacity
    slot_rank = (slot_index - slot_block * capacity).astype(jnp.float32)

    def hits(ids, base):
        mine = (ids >= base) & (ids < base + vocab_rows)
        mine_f = mine.astype(jnp.float32)
        rank = jnp.dot(
            mine_f.astype(jnp.bfloat16), earlier, preferred_element_type=jnp.float32
        )
        return mine & (rank == slot_rank)

    own_ids = jnp.broadcast_to(ids_ref[...], (slots, LANES))
    own_base = lax.rem(me - slot_block + n_dp, n_dp) * vocab_rows
    place = hits(own_ids, own_base).astype(jnp.float32).astype(jnp.bfloat16)

    for copy in ids_copies:
        copy.wait_recv()

    w_copies = [
        pltpu.make_async_copy(wq_hbm, wq_v, w_sem.at[0]),
        pltpu.make_async_copy(wkv_hbm, wkv_v, w_sem.at[1]),
        pltpu.make_async_copy(kc_hbm.at[0], kc_v, w_sem.at[2]),
        pltpu.make_async_copy(vc_hbm.at[0], vc_v, w_sem.at[3]),
    ]
    wout_copies = []
    for k in range(n_chip):
        target_chip = lax.rem(chip + k, n_chip)
        for which in range(2):
            chunk = 2 * target_chip + (parity if which else 1 - parity)
            start = pl.multiple_of(chunk * width, width)
            wout_copies.append(
                pltpu.make_async_copy(
                    wout_hbm.at[:, pl.ds(start, width)],
                    wout_v.at[2 * k + which],
                    wout_sem.at[2 * k + which],
                )
            )
    for copy in w_copies + wout_copies:
        copy.start()

    rows_ids = jnp.concatenate(
        [
            jnp.broadcast_to(ids_ref[...] if k == 0 else ids_all[k], (capacity, LANES))
            for k in range(n_dp)
        ],
        axis=0,
    )
    base = me * vocab_rows
    hit = hits(rows_ids, base)
    offset = (
        jnp.sum(
            jnp.where(hit, (rows_ids - base + 1).astype(jnp.float32), 0.0),
            axis=1,
            keepdims=True,
        )
        - 1.0
    ).astype(jnp.int32)
    for copy in table_copies:
        copy.wait()
    step = min(512, vocab_rows)
    step_lane = lax.broadcasted_iota(jnp.int32, (slots, step), 1)
    acc[...] = jnp.zeros_like(acc)

    def table_step(i, carry):
        first = pl.multiple_of(i * step, step)
        pick = ((step_lane + first) == offset).astype(jnp.float32).astype(jnp.bfloat16)
        acc[...] += jnp.dot(
            pick, table_v[pl.ds(first, step), :], preferred_element_type=jnp.float32
        )
        return carry

    lax.fori_loop(0, vocab_rows // step, table_step, 0)
    for k in range(n_dp):
        slot_send[k] = acc[k * capacity : (k + 1) * capacity, :].astype(jnp.bfloat16)
    row_copies = []
    for k in range(1, n_dp):
        back = n_dp - k
        row_copies.append(
            dp_copy(slot_send.at[k], slot_recv.at[back], row_ssem.at[k], row_rsem.at[back], back)
        )
    for copy in row_copies:
        copy.start()
    slot_recv[0] = slot_send[0]
    for k in range(1, n_dp):
        dp_copy(slot_send.at[k], slot_recv.at[k], row_ssem.at[k], row_rsem.at[k], k).wait_recv()
    arrived = slot_recv[...].reshape(slots, width)
    embedded = lax.dot_general(
        place, arrived, (((0,), (0,)), ((), ())), preferred_element_type=jnp.float32
    )[:nodes]
    emb_all[t] = embedded.astype(jnp.bfloat16)

    ag_copies = [
        t_copy(emb_all.at[t], emb_all.at[t], ag_ssem.at[k], ag_rsem.at[t],
               lax.rem(t + 2 * k, n_t) if k else partner)
        for k in range(n_chip)
    ]
    for copy in ag_copies[1:] + ag_copies[:1]:
        copy.start()

    def ag_wait(origin):
        t_copy(emb_all.at[origin], emb_all.at[origin], ag_ssem.at[0], ag_rsem.at[origin],
               partner).wait_recv()

    fw_copies = []
    for k in range(1, n_chip):
        origin = lax.rem(t - 2 * k + n_t, n_t)
        ag_wait(origin)
        copy = t_copy(emb_all.at[origin], emb_all.at[origin], fw_ssem.at[k], ag_rsem.at[origin],
                      partner)
        copy.start()
        fw_copies.append(copy)
    ag_wait(partner)
    for k in range(1, n_chip):
        ag_wait(lax.rem(partner - 2 * k + n_t, n_t))

    squares = jnp.zeros((nodes, 1), jnp.float32)
    for j in range(n_t):
        features = emb_all[j].astype(jnp.float32)
        squares = squares + jnp.sum(features * features, axis=1, keepdims=True)
    inv_rms = lax.rsqrt(squares / (n_t * width) + EPS)
    for copy in w_copies:
        copy.wait()
    queries = jnp.zeros((nodes, wq_v.shape[1]), jnp.float32)
    keys_raw = jnp.zeros((nodes, wkv_v.shape[2]), jnp.float32)
    values_raw = jnp.zeros((nodes, wkv_v.shape[2]), jnp.float32)
    for j in range(n_t):
        span = slice(j * width, (j + 1) * width)
        gain = gain_ref[:, span].astype(jnp.float32)
        normed = (emb_all[j].astype(jnp.float32) * inv_rms * gain).astype(jnp.bfloat16)
        queries = queries + jnp.dot(normed, wq_v[span, :], preferred_element_type=jnp.float32)
        keys_raw = keys_raw + jnp.dot(normed, wkv_v[0, span, :], preferred_element_type=jnp.float32)
        values_raw = values_raw + jnp.dot(
            normed, wkv_v[1, span, :], preferred_element_type=jnp.float32
        )
    values_new = values_raw.astype(jnp.bfloat16)
    cosine = cos_ref[...]
    sine = sin_ref[...]

    def rotary(values):
        return (values * cosine + pltpu.roll(values, head_dim // 2, 1) * sine).astype(jnp.bfloat16)

    scale = head_dim ** (-0.5)
    live = live_ref[...] > 0
    tree = jnp.concatenate([anc_ref[0]] * groups, axis=0) > 0
    contract = (((1,), (1,)), ((), ()))
    for kv in range(kv_local):
        cols = slice(kv * head_dim, (kv + 1) * head_dim)
        query = jnp.concatenate(
            [
                rotary(queries[:, h * head_dim : (h + 1) * head_dim])
                for h in range(kv * groups, (kv + 1) * groups)
            ],
            axis=0,
        )
        key_tree = rotary(keys_raw[:, cols])
        cache_scores = (
            lax.dot_general(query, kc_v[kv], contract, preferred_element_type=jnp.float32) * scale
        )
        cache_scores = jnp.where(live, cache_scores, NEG)
        tree_scores = (
            lax.dot_general(query, key_tree, contract, preferred_element_type=jnp.float32) * scale
        )
        tree_scores = jnp.where(tree, tree_scores, NEG)
        top = jnp.maximum(
            jnp.max(cache_scores, axis=1, keepdims=True),
            jnp.max(tree_scores, axis=1, keepdims=True),
        )
        cache_exp = jnp.exp(cache_scores - top)
        tree_exp = jnp.exp(tree_scores - top)
        denominator = jnp.sum(cache_exp, axis=1, keepdims=True) + jnp.sum(
            tree_exp, axis=1, keepdims=True
        )
        weighted = jnp.dot(
            tree_exp.astype(jnp.bfloat16), values_new[:, cols], preferred_element_type=jnp.float32
        ) + jnp.dot(cache_exp.astype(jnp.bfloat16), vc_v[kv], preferred_element_type=jnp.float32)
        context = (weighted / denominator).astype(jnp.bfloat16)
        for g in range(groups):
            h = kv * groups + g
            ctx_v[:, h * head_dim : (h + 1) * head_dim] = context[g * nodes : (g + 1) * nodes]

    for copy in wout_copies:
        copy.wait()
    contexts = ctx_v[...]
    order = list(range(1, n_chip)) + [0]
    rs1_copies = {}
    for k in order:
        part = jnp.dot(contexts, wout_v[2 * k], preferred_element_type=jnp.float32)
        rs1_send[k] = part.astype(jnp.bfloat16)
        rs1_copies[k] = t_copy(
            rs1_send.at[k], rs1_recv.at[k], rs1_ssem.at[k], rs1_rsem.at[k], partner
        )
        rs1_copies[k].start()
    rs2_copies = []
    total = None
    for k in order:
        part = jnp.dot(contexts, wout_v[2 * k + 1], preferred_element_type=jnp.float32)
        rs1_copies[k].wait_recv()
        both = part + rs1_recv[k].astype(jnp.float32)
        if k:
            rs2_send[k] = both.astype(jnp.bfloat16)
            copy = t_copy(
                rs2_send.at[k], rs2_recv.at[k], rs2_ssem.at[k], rs2_rsem.at[k],
                lax.rem(t + 2 * k, n_t),
            )
            copy.start()
            rs2_copies.append(copy)
        else:
            total = both
    total = total + emb_all[t].astype(jnp.float32)
    for k, copy in enumerate(rs2_copies):
        copy.wait_recv()
        total = total + rs2_recv[k + 1].astype(jnp.float32)
    out_ref[...] = total.astype(jnp.bfloat16)
    for copy in (
        ids_copies + row_copies + ag_copies + fw_copies + list(rs1_copies.values()) + rs2_copies
    ):
        copy.wait_send()


def shards(tree_ids, ancestors, lengths, table, gain, w_query, w_kv, w_out, key_cache, value_cache):
    n_dp = lax.axis_size("dp")
    n_t = lax.axis_size("tensor")
    n_chip = n_t // 2
    row_count, nodes = tree_ids.shape
    vocab_rows, width = table.shape
    head_dim = key_cache.shape[3]
    context = key_cache.shape[2]
    kv_local = key_cache.shape[1]
    capacity = 2 * ((row_count * nodes + n_dp - 1) // n_dp)
    capacity = 16 * ((capacity + 15) // 16)
    ids = jnp.pad(tree_ids, ((0, 0), (0, LANES - nodes)), constant_values=-1)
    half_dim = head_dim // 2
    inverse = jnp.exp(
        jnp.arange(half_dim, dtype=jnp.float32) * (-2.0 * math.log(THETA) / head_dim)
    )
    positions = (lengths[:, None] + jnp.sum(ancestors, axis=2) - 1).reshape(-1)
    angles = positions.astype(jnp.float32)[:, None] * inverse[None, :]
    cosine = jnp.cos(angles)
    sine = jnp.sin(angles)
    cosine = jnp.concatenate([cosine, cosine], axis=1)
    sine = jnp.concatenate([-sine, sine], axis=1)
    live = (jnp.arange(context, dtype=jnp.int32)[None, :] < lengths[:, None]).astype(jnp.int32)
    bf16, f32 = jnp.bfloat16, jnp.float32
    n_tab = 4
    sems = pltpu.SemaphoreType.DMA
    vmem = pl.BlockSpec(memory_space=pltpu.VMEM)
    hbm = pl.BlockSpec(memory_space=pl.ANY)
    return pl.pallas_call(
        functools.partial(layer_kernel, n_dp, n_t, nodes, capacity),
        out_shape=jax.ShapeDtypeStruct((nodes, width), bf16),
        in_specs=[vmem] * 6 + [hbm] * 6,
        out_specs=vmem,
        scratch_shapes=[
            pltpu.VMEM((n_dp, 1, LANES), jnp.int32),
            pltpu.VMEM(table.shape, bf16),
            pltpu.VMEM(w_query.shape, bf16),
            pltpu.VMEM(w_kv.shape, bf16),
            pltpu.VMEM((n_t, w_out.shape[0], width), bf16),
            pltpu.VMEM(key_cache.shape[1:], bf16),
            pltpu.VMEM(value_cache.shape[1:], bf16),
            pltpu.VMEM((n_dp * capacity, width), f32),
            pltpu.VMEM((n_dp, capacity, width), bf16),
            pltpu.VMEM((n_dp, capacity, width), bf16),
            pltpu.VMEM((n_t, nodes, width), bf16),
            pltpu.VMEM((nodes, w_query.shape[1]), bf16),
            pltpu.VMEM((n_chip, nodes, width), bf16),
            pltpu.VMEM((n_chip, nodes, width), bf16),
            pltpu.VMEM((n_chip, nodes, width), bf16),
            pltpu.VMEM((n_chip, nodes, width), bf16),
            sems((n_tab,)),
            sems((4,)),
            sems((n_t,)),
            sems((n_dp,)),
            sems((n_dp,)),
            sems((n_dp,)),
            sems((n_dp,)),
            sems((1,)),
            sems((n_chip,)),
            sems((n_t,)),
            sems((n_chip,)),
            sems((n_chip,)),
            sems((n_chip,)),
            sems((n_chip,)),
            sems((n_chip,)),
        ],
        compiler_params=pltpu.CompilerParams(
            collective_id=0, has_side_effects=True, vmem_limit_bytes=62 * 1024 * 1024
        ),
    )(
        ids,
        ancestors,
        live,
        cosine,
        sine,
        gain.reshape(1, -1),
        table,
        w_query,
        w_kv,
        w_out,
        key_cache,
        value_cache,
    )


def solution(mesh):
    in_specs = (
        P("dp", None),
        P("dp", None, None),
        P("dp"),
        P("dp", "tensor"),
        P(),
        P(None, "tensor"),
        P(None, None, "tensor"),
        P("tensor", None),
        P("dp", "tensor", None, None),
        P("dp", "tensor", None, None),
    )
    out_specs = P("dp", "tensor")
    return jax.shard_map(shards, mesh=mesh, in_specs=in_specs, out_specs=out_specs, check_vma=False)
```

```python
import functools
import math

import jax
import jax.numpy as jnp
from jax import lax
from jax.experimental import pallas as pl
from jax.experimental.pallas import tpu as pltpu
from jax.sharding import PartitionSpec as P

EPS = 1e-05
NEG = -1e30
THETA = 500000.0
MESH = pl.DeviceIdType.MESH


def layer_kernel(
    n_dp,
    n_t,
    nodes,
    capacity,
    ids_ref,
    anc_ref,
    len_ref,
    gain_ref,
    table_hbm,
    wq_hbm,
    wkv_hbm,
    wout_hbm,
    kc_hbm,
    vc_hbm,
    out_ref,
    ids_all,
    cos_v,
    sin_v,
    table_v,
    wq_v,
    wkv_v,
    wout_v,
    kc_v,
    vc_v,
    acc,
    slot_send,
    slot_recv,
    emb_all,
    ctx_v,
    rs1_send,
    rs1_recv,
    rs2_send,
    rs2_recv,
    table_sem,
    w_sem,
    wout_sem,
    ids_ssem,
    ids_rsem,
    row_ssem,
    row_rsem,
    own_sem,
    ag_ssem,
    ag_rsem,
    fw_ssem,
    rs1_ssem,
    rs1_rsem,
    rs2_ssem,
    rs2_rsem,
):
    me = lax.axis_index("dp")
    t = lax.axis_index("tensor")
    chip = t // 2
    parity = t % 2
    partner = t + 1 - 2 * parity
    n_chip = n_t // 2
    vocab_rows, width = table_v.shape
    head_dim = kc_v.shape[-1]
    kv_local = kc_v.shape[0]
    heads = wq_v.shape[1] // head_dim
    groups = heads // kv_local
    slots = n_dp * capacity

    barrier = pltpu.get_barrier_semaphore()
    for k in range(1, n_dp):
        pl.semaphore_signal(
            barrier, inc=1, device_id={"dp": lax.rem(me + k, n_dp)}, device_id_type=MESH
        )
    for k in range(1, n_t):
        pl.semaphore_signal(
            barrier, inc=1, device_id={"tensor": lax.rem(t + k, n_t)}, device_id_type=MESH
        )
    n_tab = table_sem.shape[0]
    tab_step = vocab_rows // n_tab
    table_copies = [
        pltpu.make_async_copy(
            table_hbm.at[pl.ds(i * tab_step, tab_step)],
            table_v.at[pl.ds(i * tab_step, tab_step)],
            table_sem.at[i],
        )
        for i in range(n_tab)
    ]
    for copy in table_copies:
        copy.start()

    pl.semaphore_wait(barrier, n_dp + n_t - 2)

    def dp_copy(src, dst, ssem, rsem, k):
        return pltpu.make_async_remote_copy(
            src_ref=src,
            dst_ref=dst,
            send_sem=ssem,
            recv_sem=rsem,
            device_id={"dp": lax.rem(me + k, n_dp)},
            device_id_type=MESH,
        )

    def t_copy(src, dst, ssem, rsem, target):
        return pltpu.make_async_remote_copy(
            src_ref=src,
            dst_ref=dst,
            send_sem=ssem,
            recv_sem=rsem,
            device_id={"tensor": target},
            device_id_type=MESH,
        )

    ids_copies = [
        dp_copy(ids_ref, ids_all.at[k], ids_ssem.at[k], ids_rsem.at[k], k)
        for k in range(1, n_dp)
    ]
    for copy in ids_copies:
        copy.start()

    sub = lax.broadcasted_iota(jnp.int32, (nodes, nodes), 0)
    lane = lax.broadcasted_iota(jnp.int32, (nodes, nodes), 1)
    earlier = (sub < lane).astype(jnp.float32).astype(jnp.bfloat16)
    slot_index = lax.broadcasted_iota(jnp.int32, (slots, nodes), 0)
    slot_block = slot_index // capacity
    slot_rank = (slot_index - slot_block * capacity).astype(jnp.float32)

    def hits(ids, base):
        mine = (ids >= base) & (ids < base + vocab_rows)
        mine_f = mine.astype(jnp.float32)
        rank = jnp.dot(
            mine_f.astype(jnp.bfloat16), earlier, preferred_element_type=jnp.float32
        )
        return mine & (rank == slot_rank)

    own_ids = jnp.broadcast_to(ids_ref[...], (slots, nodes))
    own_base = lax.rem(me - slot_block + n_dp, n_dp) * vocab_rows
    place = hits(own_ids, own_base).astype(jnp.float32).astype(jnp.bfloat16)

    depth = jnp.sum(anc_ref[0].astype(jnp.float32), axis=1, keepdims=True)
    positions = depth + (len_ref[0] - 1).astype(jnp.float32)
    half_dim = head_dim // 2
    lanes = lax.broadcasted_iota(jnp.int32, (1, head_dim), 1)
    freq_index = jnp.where(lanes < half_dim, lanes, lanes - half_dim).astype(jnp.float32)
    angles = positions * jnp.exp(freq_index * (-2.0 * math.log(THETA) / head_dim))
    cosine = jnp.cos(angles)
    sine = jnp.where(lanes < half_dim, -jnp.sin(angles), jnp.sin(angles))
    cos_v[...] = cosine
    sin_v[...] = sine

    for copy in ids_copies:
        copy.wait_recv()

    w_copies = [
        pltpu.make_async_copy(wq_hbm, wq_v, w_sem.at[0]),
        pltpu.make_async_copy(wkv_hbm, wkv_v, w_sem.at[1]),
        pltpu.make_async_copy(kc_hbm.at[0], kc_v, w_sem.at[2]),
        pltpu.make_async_copy(vc_hbm.at[0], vc_v, w_sem.at[3]),
    ]
    wout_copies = []
    for k in range(n_chip):
        target_chip = lax.rem(chip + k, n_chip)
        for which in range(2):
            chunk = 2 * target_chip + (parity if which else 1 - parity)
            start = pl.multiple_of(chunk * width, width)
            wout_copies.append(
                pltpu.make_async_copy(
                    wout_hbm.at[:, pl.ds(start, width)],
                    wout_v.at[2 * k + which],
                    wout_sem.at[2 * k + which],
                )
            )
    for copy in w_copies + wout_copies:
        copy.start()

    rows_ids = jnp.concatenate(
        [
            jnp.broadcast_to(ids_ref[...] if k == 0 else ids_all[k], (capacity, nodes))
            for k in range(n_dp)
        ],
        axis=0,
    )
    base = me * vocab_rows
    hit = hits(rows_ids, base)
    offset = (
        jnp.sum(
            jnp.where(hit, (rows_ids - base + 1).astype(jnp.float32), 0.0),
            axis=1,
            keepdims=True,
        )
        - 1.0
    ).astype(jnp.int32)
    for copy in table_copies:
        copy.wait()
    step = min(512, vocab_rows)
    step_lane = lax.broadcasted_iota(jnp.int32, (slots, step), 1)
    acc[...] = jnp.zeros_like(acc)

    def table_step(i, carry):
        first = pl.multiple_of(i * step, step)
        pick = ((step_lane + first) == offset).astype(jnp.float32).astype(jnp.bfloat16)
        acc[...] += jnp.dot(
            pick, table_v[pl.ds(first, step), :], preferred_element_type=jnp.float32
        )
        return carry

    lax.fori_loop(0, vocab_rows // step, table_step, 0)
    for k in range(n_dp):
        slot_send[k] = acc[k * capacity : (k + 1) * capacity, :].astype(jnp.bfloat16)
    row_copies = []
    for k in range(1, n_dp):
        back = n_dp - k
        row_copies.append(
            dp_copy(slot_send.at[k], slot_recv.at[back], row_ssem.at[k], row_rsem.at[back], back)
        )
    for copy in row_copies:
        copy.start()
    slot_recv[0] = slot_send[0]
    for k in range(1, n_dp):
        dp_copy(slot_send.at[k], slot_recv.at[k], row_ssem.at[k], row_rsem.at[k], k).wait_recv()
    arrived = slot_recv[...].reshape(slots, width)
    embedded = lax.dot_general(
        place, arrived, (((0,), (0,)), ((), ())), preferred_element_type=jnp.float32
    )[:nodes]
    emb_all[t] = embedded.astype(jnp.bfloat16)

    ag_copies = [
        t_copy(emb_all.at[t], emb_all.at[t], ag_ssem.at[k], ag_rsem.at[t],
               lax.rem(t + 2 * k, n_t) if k else partner)
        for k in range(n_chip)
    ]
    for copy in ag_copies[1:] + ag_copies[:1]:
        copy.start()

    def ag_wait(origin):
        t_copy(emb_all.at[origin], emb_all.at[origin], ag_ssem.at[0], ag_rsem.at[origin],
               partner).wait_recv()

    fw_copies = []
    for k in range(1, n_chip):
        origin = lax.rem(t - 2 * k + n_t, n_t)
        ag_wait(origin)
        copy = t_copy(emb_all.at[origin], emb_all.at[origin], fw_ssem.at[k], ag_rsem.at[origin],
                      partner)
        copy.start()
        fw_copies.append(copy)
    ag_wait(partner)
    for k in range(1, n_chip):
        ag_wait(lax.rem(partner - 2 * k + n_t, n_t))

    squares = jnp.zeros((nodes, 1), jnp.float32)
    for j in range(n_t):
        features = emb_all[j].astype(jnp.float32)
        squares = squares + jnp.sum(features * features, axis=1, keepdims=True)
    inv_rms = lax.rsqrt(squares / (n_t * width) + EPS)
    for copy in w_copies:
        copy.wait()
    queries = jnp.zeros((nodes, wq_v.shape[1]), jnp.float32)
    keys_raw = jnp.zeros((nodes, wkv_v.shape[2]), jnp.float32)
    values_raw = jnp.zeros((nodes, wkv_v.shape[2]), jnp.float32)
    for j in range(n_t):
        span = slice(j * width, (j + 1) * width)
        gain = gain_ref[span].astype(jnp.float32)[None, :]
        normed = (emb_all[j].astype(jnp.float32) * inv_rms * gain).astype(jnp.bfloat16)
        queries = queries + jnp.dot(normed, wq_v[span, :], preferred_element_type=jnp.float32)
        keys_raw = keys_raw + jnp.dot(normed, wkv_v[0, span, :], preferred_element_type=jnp.float32)
        values_raw = values_raw + jnp.dot(
            normed, wkv_v[1, span, :], preferred_element_type=jnp.float32
        )
    values_new = values_raw.astype(jnp.bfloat16)
    cosine = cos_v[...]
    sine = sin_v[...]

    def rotary(values):
        return (values * cosine + pltpu.roll(values, head_dim // 2, 1) * sine).astype(jnp.bfloat16)

    scale = head_dim ** (-0.5)
    live = lax.broadcasted_iota(jnp.int32, (1, kc_v.shape[1]), 1) < len_ref[0]
    tree = jnp.concatenate([anc_ref[0]] * groups, axis=0) > 0
    contract = (((1,), (1,)), ((), ()))
    for kv in range(kv_local):
        cols = slice(kv * head_dim, (kv + 1) * head_dim)
        query = jnp.concatenate(
            [
                rotary(queries[:, h * head_dim : (h + 1) * head_dim])
                for h in range(kv * groups, (kv + 1) * groups)
            ],
            axis=0,
        )
        key_tree = rotary(keys_raw[:, cols])
        cache_scores = (
            lax.dot_general(query, kc_v[kv], contract, preferred_element_type=jnp.float32) * scale
        )
        cache_scores = jnp.where(live, cache_scores, NEG)
        tree_scores = (
            lax.dot_general(query, key_tree, contract, preferred_element_type=jnp.float32) * scale
        )
        tree_scores = jnp.where(tree, tree_scores, NEG)
        top = jnp.maximum(
            jnp.max(cache_scores, axis=1, keepdims=True),
            jnp.max(tree_scores, axis=1, keepdims=True),
        )
        cache_exp = jnp.exp(cache_scores - top)
        tree_exp = jnp.exp(tree_scores - top)
        denominator = jnp.sum(cache_exp, axis=1, keepdims=True) + jnp.sum(
            tree_exp, axis=1, keepdims=True
        )
        weighted = jnp.dot(
            tree_exp.astype(jnp.bfloat16), values_new[:, cols], preferred_element_type=jnp.float32
        ) + jnp.dot(cache_exp.astype(jnp.bfloat16), vc_v[kv], preferred_element_type=jnp.float32)
        context = (weighted / denominator).astype(jnp.bfloat16)
        for g in range(groups):
            h = kv * groups + g
            ctx_v[:, h * head_dim : (h + 1) * head_dim] = context[g * nodes : (g + 1) * nodes]

    for copy in wout_copies:
        copy.wait()
    contexts = ctx_v[...]
    order = list(range(1, n_chip)) + [0]
    rs1_copies = {}
    for k in order:
        part = jnp.dot(contexts, wout_v[2 * k], preferred_element_type=jnp.float32)
        rs1_send[k] = part.astype(jnp.bfloat16)
        rs1_copies[k] = t_copy(
            rs1_send.at[k], rs1_recv.at[k], rs1_ssem.at[k], rs1_rsem.at[k], partner
        )
        rs1_copies[k].start()
    rs2_copies = []
    total = None
    for k in order:
        part = jnp.dot(contexts, wout_v[2 * k + 1], preferred_element_type=jnp.float32)
        rs1_copies[k].wait_recv()
        both = part + rs1_recv[k].astype(jnp.float32)
        if k:
            rs2_send[k] = both.astype(jnp.bfloat16)
            copy = t_copy(
                rs2_send.at[k], rs2_recv.at[k], rs2_ssem.at[k], rs2_rsem.at[k],
                lax.rem(t + 2 * k, n_t),
            )
            copy.start()
            rs2_copies.append(copy)
        else:
            total = both
    total = total + emb_all[t].astype(jnp.float32)
    for k, copy in enumerate(rs2_copies):
        copy.wait_recv()
        total = total + rs2_recv[k + 1].astype(jnp.float32)
    out_ref[...] = total
    for copy in (
        ids_copies + row_copies + ag_copies + fw_copies + list(rs1_copies.values()) + rs2_copies
    ):
        copy.wait_send()


def shards(tree_ids, ancestors, lengths, table, gain, w_query, w_kv, w_out, key_cache, value_cache):
    n_dp = lax.axis_size("dp")
    n_t = lax.axis_size("tensor")
    n_chip = n_t // 2
    row_count, nodes = tree_ids.shape
    vocab_rows, width = table.shape
    head_dim = key_cache.shape[3]
    capacity = 2 * ((row_count * nodes + n_dp - 1) // n_dp)
    capacity = 16 * ((capacity + 15) // 16)
    bf16, f32 = jnp.bfloat16, jnp.float32
    n_tab = 4
    sems = pltpu.SemaphoreType.DMA
    vmem = pl.BlockSpec(memory_space=pltpu.VMEM)
    hbm = pl.BlockSpec(memory_space=pl.ANY)
    return pl.pallas_call(
        functools.partial(layer_kernel, n_dp, n_t, nodes, capacity),
        out_shape=jax.ShapeDtypeStruct((nodes, width), f32),
        in_specs=[vmem, vmem, pl.BlockSpec(memory_space=pltpu.SMEM), vmem] + [hbm] * 6,
        out_specs=vmem,
        scratch_shapes=[
            pltpu.VMEM((n_dp, 1, nodes), jnp.int32),
            pltpu.VMEM((nodes, head_dim), f32),
            pltpu.VMEM((nodes, head_dim), f32),
            pltpu.VMEM(table.shape, bf16),
            pltpu.VMEM(w_query.shape, bf16),
            pltpu.VMEM(w_kv.shape, bf16),
            pltpu.VMEM((n_t, w_out.shape[0], width), bf16),
            pltpu.VMEM(key_cache.shape[1:], bf16),
            pltpu.VMEM(value_cache.shape[1:], bf16),
            pltpu.VMEM((n_dp * capacity, width), f32),
            pltpu.VMEM((n_dp, capacity, width), bf16),
            pltpu.VMEM((n_dp, capacity, width), bf16),
            pltpu.VMEM((n_t, nodes, width), bf16),
            pltpu.VMEM((nodes, w_query.shape[1]), bf16),
            pltpu.VMEM((n_chip, nodes, width), bf16),
            pltpu.VMEM((n_chip, nodes, width), bf16),
            pltpu.VMEM((n_chip, nodes, width), bf16),
            pltpu.VMEM((n_chip, nodes, width), bf16),
            sems((n_tab,)),
            sems((4,)),
            sems((n_t,)),
            sems((n_dp,)),
            sems((n_dp,)),
            sems((n_dp,)),
            sems((n_dp,)),
            sems((1,)),
            sems((n_chip,)),
            sems((n_t,)),
            sems((n_chip,)),
            sems((n_chip,)),
            sems((n_chip,)),
            sems((n_chip,)),
            sems((n_chip,)),
        ],
        compiler_params=pltpu.CompilerParams(
            collective_id=0, has_side_effects=True, vmem_limit_bytes=62 * 1024 * 1024
        ),
    )(
        tree_ids,
        ancestors,
        lengths,
        gain,
        table,
        w_query,
        w_kv,
        w_out,
        key_cache,
        value_cache,
    ).astype(bf16)


def solution(mesh):
    in_specs = (
        P("dp", None),
        P("dp", None, None),
        P("dp"),
        P("dp", "tensor"),
        P(),
        P(None, "tensor"),
        P(None, None, "tensor"),
        P("tensor", None),
        P("dp", "tensor", None, None),
        P("dp", "tensor", None, None),
    )
    out_specs = P("dp", "tensor")
    return jax.shard_map(shards, mesh=mesh, in_specs=in_specs, out_specs=out_specs, check_vma=False)
```

```python
import functools
import math

import jax
import jax.numpy as jnp
from jax import lax
from jax.experimental import pallas as pl
from jax.experimental.pallas import tpu as pltpu
from jax.sharding import PartitionSpec as P

EPS = 1e-05
NEG = -1e30
THETA = 500000.0
MESH = pl.DeviceIdType.MESH


def layer_kernel(
    n_dp,
    n_t,
    nodes,
    capacity,
    ids_ref,
    anc_ref,
    len_ref,
    gain_ref,
    table_hbm,
    wq_hbm,
    wkv_hbm,
    wout_hbm,
    kc_hbm,
    vc_hbm,
    out_ref,
    ids_all,
    cos_v,
    sin_v,
    table_v,
    wq_v,
    wkv_v,
    wout_v,
    kc_v,
    vc_v,
    pick_v,
    slot_send,
    slot_recv,
    emb_all,
    ctx_v,
    rs1_send,
    rs1_recv,
    rs2_send,
    rs2_recv,
    table_sem,
    w_sem,
    wout_sem,
    ids_ssem,
    ids_rsem,
    row_ssem,
    row_rsem,
    ag_ssem,
    ag_rsem,
    fw_ssem,
    rs1_ssem,
    rs1_rsem,
    rs2_ssem,
    rs2_rsem,
):
    me = lax.axis_index("dp")
    t = lax.axis_index("tensor")
    chip = t // 2
    parity = t % 2
    partner = t + 1 - 2 * parity
    n_chip = n_t // 2
    vocab_rows, width = table_v.shape
    head_dim = kc_v.shape[-1]
    kv_local = kc_v.shape[0]
    heads = wq_v.shape[1] // head_dim
    groups = heads // kv_local
    slots = n_dp * capacity
    n_part = emb_all.shape[0]
    part_width = width // n_part

    barrier = pltpu.get_barrier_semaphore()
    for k in range(1, n_dp):
        pl.semaphore_signal(
            barrier, inc=1, device_id={"dp": lax.rem(me + k, n_dp)}, device_id_type=MESH
        )
    for k in range(1, n_t):
        pl.semaphore_signal(
            barrier, inc=1, device_id={"tensor": lax.rem(t + k, n_t)}, device_id_type=MESH
        )
    n_tab = table_sem.shape[0]
    tab_step = vocab_rows // n_tab
    table_copies = [
        pltpu.make_async_copy(
            table_hbm.at[pl.ds(i * tab_step, tab_step)],
            table_v.at[pl.ds(i * tab_step, tab_step)],
            table_sem.at[i],
        )
        for i in range(n_tab)
    ]
    for copy in table_copies:
        copy.start()

    pl.semaphore_wait(barrier, n_dp + n_t - 2)

    def dp_copy(src, dst, ssem, rsem, k):
        return pltpu.make_async_remote_copy(
            src_ref=src,
            dst_ref=dst,
            send_sem=ssem,
            recv_sem=rsem,
            device_id={"dp": lax.rem(me + k, n_dp)},
            device_id_type=MESH,
        )

    def t_copy(src, dst, ssem, rsem, target):
        return pltpu.make_async_remote_copy(
            src_ref=src,
            dst_ref=dst,
            send_sem=ssem,
            recv_sem=rsem,
            device_id={"tensor": target},
            device_id_type=MESH,
        )

    ids_copies = [
        dp_copy(ids_ref, ids_all.at[k], ids_ssem.at[k], ids_rsem.at[k], k)
        for k in range(1, n_dp)
    ]
    for copy in ids_copies:
        copy.start()

    sub = lax.broadcasted_iota(jnp.int32, (nodes, nodes), 0)
    lane = lax.broadcasted_iota(jnp.int32, (nodes, nodes), 1)
    earlier = (sub < lane).astype(jnp.float32).astype(jnp.bfloat16)
    slot_index = lax.broadcasted_iota(jnp.int32, (slots, nodes), 0)
    slot_block = slot_index // capacity
    slot_rank = (slot_index - slot_block * capacity).astype(jnp.float32)

    def hits(ids, base):
        mine = (ids >= base) & (ids < base + vocab_rows)
        mine_f = mine.astype(jnp.float32)
        rank = jnp.dot(
            mine_f.astype(jnp.bfloat16), earlier, preferred_element_type=jnp.float32
        )
        return mine & (rank == slot_rank)

    own_ids = jnp.broadcast_to(ids_ref[...], (slots, nodes))
    own_base = lax.rem(me - slot_block + n_dp, n_dp) * vocab_rows
    place = hits(own_ids, own_base).astype(jnp.float32).astype(jnp.bfloat16)

    depth = jnp.sum(anc_ref[0].astype(jnp.float32), axis=1, keepdims=True)
    positions = depth + (len_ref[0] - 1).astype(jnp.float32)
    half_dim = head_dim // 2
    lanes = lax.broadcasted_iota(jnp.int32, (1, head_dim), 1)
    freq_index = jnp.where(lanes < half_dim, lanes, lanes - half_dim).astype(jnp.float32)
    angles = positions * jnp.exp(freq_index * (-2.0 * math.log(THETA) / head_dim))
    cosine = jnp.cos(angles)
    sine = jnp.where(lanes < half_dim, -jnp.sin(angles), jnp.sin(angles))
    cos_v[...] = cosine
    sin_v[...] = sine

    for copy in ids_copies:
        copy.wait_recv()

    w_copies = [
        pltpu.make_async_copy(wq_hbm, wq_v, w_sem.at[0]),
        pltpu.make_async_copy(wkv_hbm, wkv_v, w_sem.at[1]),
        pltpu.make_async_copy(kc_hbm.at[0], kc_v, w_sem.at[2]),
        pltpu.make_async_copy(vc_hbm.at[0], vc_v, w_sem.at[3]),
    ]
    wout_copies = []
    for k in range(n_chip):
        target_chip = lax.rem(chip + k, n_chip)
        for which in range(2):
            chunk = 2 * target_chip + (parity if which else 1 - parity)
            start = pl.multiple_of(chunk * width, width)
            wout_copies.append(
                pltpu.make_async_copy(
                    wout_hbm.at[:, pl.ds(start, width)],
                    wout_v.at[2 * k + which],
                    wout_sem.at[2 * k + which],
                )
            )
    for copy in w_copies + wout_copies:
        copy.start()

    rows_ids = jnp.concatenate(
        [
            jnp.broadcast_to(ids_ref[...] if k == 0 else ids_all[k], (capacity, nodes))
            for k in range(n_dp)
        ],
        axis=0,
    )
    base = me * vocab_rows
    hit = hits(rows_ids, base)
    offset = (
        jnp.sum(
            jnp.where(hit, (rows_ids - base + 1).astype(jnp.float32), 0.0),
            axis=1,
            keepdims=True,
        )
        - 1.0
    ).astype(jnp.int32)
    step = min(512, vocab_rows)
    step_lane = lax.broadcasted_iota(jnp.int32, (slots, step), 1)
    for i in range(vocab_rows // step):
        pick_v[i] = ((step_lane + i * step) == offset).astype(jnp.float32).astype(jnp.bfloat16)
    for copy in table_copies:
        copy.wait()

    row_copies = []
    for q in range(n_part):

        def table_step(i, total, q=q):
            first = pl.multiple_of(i * step, step)
            return total + jnp.dot(
                pick_v[i],
                table_v[pl.ds(first, step), q * part_width : (q + 1) * part_width],
                preferred_element_type=jnp.float32,
            )

        picked = lax.fori_loop(
            0, vocab_rows // step, table_step, jnp.zeros((slots, part_width), jnp.float32)
        ).astype(jnp.bfloat16)
        for k in range(n_dp):
            slot_send[q, k] = picked[k * capacity : (k + 1) * capacity, :]
        for k in range(1, n_dp):
            back = n_dp - k
            copy = dp_copy(
                slot_send.at[q, k],
                slot_recv.at[q, back],
                row_ssem.at[q, k],
                row_rsem.at[q, back],
                back,
            )
            copy.start()
            row_copies.append(copy)
        slot_recv[q, 0] = slot_send[q, 0]

    def ag_copy(q, origin, ssem, target):
        return t_copy(
            emb_all.at[q, origin], emb_all.at[q, origin], ssem, ag_rsem.at[q, origin], target
        )

    ag_copies = []
    fw_copies = []

    def forward(q):
        for k in range(1, n_chip):
            origin = lax.rem(t - 2 * k + n_t, n_t)
            copy = ag_copy(q, origin, fw_ssem.at[q, k], partner)
            copy.wait_recv()
            copy.start()
            fw_copies.append(copy)

    for q in range(n_part):
        for k in range(1, n_dp):
            dp_copy(
                slot_send.at[q, k], slot_recv.at[q, k], row_ssem.at[q, k], row_rsem.at[q, k], k
            ).wait_recv()
        arrived = slot_recv[q].reshape(slots, part_width)
        embedded = lax.dot_general(
            place, arrived, (((0,), (0,)), ((), ())), preferred_element_type=jnp.float32
        )
        emb_all[q, t] = embedded.astype(jnp.bfloat16)
        for k in list(range(1, n_chip)) + [0]:
            copy = ag_copy(q, t, ag_ssem.at[q, k], lax.rem(t + 2 * k, n_t) if k else partner)
            copy.start()
            ag_copies.append(copy)
        if q:
            forward(q - 1)
    forward(n_part - 1)
    for q in range(n_part):
        ag_copy(q, partner, ag_ssem.at[q, 0], partner).wait_recv()
        for k in range(1, n_chip):
            origin = lax.rem(partner - 2 * k + n_t, n_t)
            ag_copy(q, origin, ag_ssem.at[q, 0], partner).wait_recv()

    squares = jnp.zeros((nodes, 1), jnp.float32)
    for j in range(n_t):
        for q in range(n_part):
            features = emb_all[q, j].astype(jnp.float32)
            squares = squares + jnp.sum(features * features, axis=1, keepdims=True)
    inv_rms = lax.rsqrt(squares / (n_t * width) + EPS)
    for copy in w_copies:
        copy.wait()
    queries = jnp.zeros((nodes, wq_v.shape[1]), jnp.float32)
    keys_raw = jnp.zeros((nodes, wkv_v.shape[2]), jnp.float32)
    values_raw = jnp.zeros((nodes, wkv_v.shape[2]), jnp.float32)
    for j in range(n_t):
        span = slice(j * width, (j + 1) * width)
        gain = gain_ref[span].astype(jnp.float32)[None, :]
        features = jnp.concatenate([emb_all[q, j] for q in range(n_part)], axis=1)
        normed = (features.astype(jnp.float32) * inv_rms * gain).astype(jnp.bfloat16)
        queries = queries + jnp.dot(normed, wq_v[span, :], preferred_element_type=jnp.float32)
        keys_raw = keys_raw + jnp.dot(normed, wkv_v[0, span, :], preferred_element_type=jnp.float32)
        values_raw = values_raw + jnp.dot(
            normed, wkv_v[1, span, :], preferred_element_type=jnp.float32
        )
    values_new = values_raw.astype(jnp.bfloat16)
    cosine = cos_v[...]
    sine = sin_v[...]

    def rotary(values):
        return (values * cosine + pltpu.roll(values, head_dim // 2, 1) * sine).astype(jnp.bfloat16)

    scale = head_dim ** (-0.5)
    live = lax.broadcasted_iota(jnp.int32, (1, kc_v.shape[1]), 1) < len_ref[0]
    tree = jnp.concatenate([anc_ref[0]] * groups, axis=0) > 0
    contract = (((1,), (1,)), ((), ()))
    for kv in range(kv_local):
        cols = slice(kv * head_dim, (kv + 1) * head_dim)
        query = jnp.concatenate(
            [
                rotary(queries[:, h * head_dim : (h + 1) * head_dim])
                for h in range(kv * groups, (kv + 1) * groups)
            ],
            axis=0,
        )
        key_tree = rotary(keys_raw[:, cols])
        cache_scores = (
            lax.dot_general(query, kc_v[kv], contract, preferred_element_type=jnp.float32) * scale
        )
        cache_scores = jnp.where(live, cache_scores, NEG)
        tree_scores = (
            lax.dot_general(query, key_tree, contract, preferred_element_type=jnp.float32) * scale
        )
        tree_scores = jnp.where(tree, tree_scores, NEG)
        top = jnp.maximum(
            jnp.max(cache_scores, axis=1, keepdims=True),
            jnp.max(tree_scores, axis=1, keepdims=True),
        )
        cache_exp = jnp.exp(cache_scores - top)
        tree_exp = jnp.exp(tree_scores - top)
        denominator = jnp.sum(cache_exp, axis=1, keepdims=True) + jnp.sum(
            tree_exp, axis=1, keepdims=True
        )
        weighted = jnp.dot(
            tree_exp.astype(jnp.bfloat16), values_new[:, cols], preferred_element_type=jnp.float32
        ) + jnp.dot(cache_exp.astype(jnp.bfloat16), vc_v[kv], preferred_element_type=jnp.float32)
        context = (weighted / denominator).astype(jnp.bfloat16)
        for g in range(groups):
            h = kv * groups + g
            ctx_v[:, h * head_dim : (h + 1) * head_dim] = context[g * nodes : (g + 1) * nodes]

    for copy in wout_copies:
        copy.wait()
    contexts = ctx_v[...]
    order = list(range(1, n_chip)) + [0]
    rs1_copies = {}
    for k in order:
        part = jnp.dot(contexts, wout_v[2 * k], preferred_element_type=jnp.float32)
        rs1_send[k] = part.astype(jnp.bfloat16)
        rs1_copies[k] = t_copy(
            rs1_send.at[k], rs1_recv.at[k], rs1_ssem.at[k], rs1_rsem.at[k], partner
        )
        rs1_copies[k].start()
    rs2_copies = []
    total = None
    for k in order:
        part = jnp.dot(contexts, wout_v[2 * k + 1], preferred_element_type=jnp.float32)
        rs1_copies[k].wait_recv()
        both = part + rs1_recv[k].astype(jnp.float32)
        if k:
            rs2_send[k] = both.astype(jnp.bfloat16)
            copy = t_copy(
                rs2_send.at[k], rs2_recv.at[k], rs2_ssem.at[k], rs2_rsem.at[k],
                lax.rem(t + 2 * k, n_t),
            )
            copy.start()
            rs2_copies.append(copy)
        else:
            total = both
    total = total + jnp.concatenate(
        [emb_all[q, t].astype(jnp.float32) for q in range(n_part)], axis=1
    )
    for k, copy in enumerate(rs2_copies):
        copy.wait_recv()
        total = total + rs2_recv[k + 1].astype(jnp.float32)
    out_ref[...] = total
    for copy in (
        ids_copies + row_copies + ag_copies + fw_copies + list(rs1_copies.values()) + rs2_copies
    ):
        copy.wait_send()


def shards(tree_ids, ancestors, lengths, table, gain, w_query, w_kv, w_out, key_cache, value_cache):
    n_dp = lax.axis_size("dp")
    n_t = lax.axis_size("tensor")
    n_chip = n_t // 2
    row_count, nodes = tree_ids.shape
    vocab_rows, width = table.shape
    head_dim = key_cache.shape[3]
    capacity = 2 * ((row_count * nodes + n_dp - 1) // n_dp)
    capacity = 16 * ((capacity + 15) // 16)
    bf16, f32 = jnp.bfloat16, jnp.float32
    n_tab = 4
    n_part = 2
    step = min(512, vocab_rows)
    sems = pltpu.SemaphoreType.DMA
    vmem = pl.BlockSpec(memory_space=pltpu.VMEM)
    hbm = pl.BlockSpec(memory_space=pl.ANY)
    return pl.pallas_call(
        functools.partial(layer_kernel, n_dp, n_t, nodes, capacity),
        out_shape=jax.ShapeDtypeStruct((nodes, width), f32),
        in_specs=[vmem, vmem, pl.BlockSpec(memory_space=pltpu.SMEM), vmem] + [hbm] * 6,
        out_specs=vmem,
        scratch_shapes=[
            pltpu.VMEM((n_dp, 1, nodes), jnp.int32),
            pltpu.VMEM((nodes, head_dim), f32),
            pltpu.VMEM((nodes, head_dim), f32),
            pltpu.VMEM(table.shape, bf16),
            pltpu.VMEM(w_query.shape, bf16),
            pltpu.VMEM(w_kv.shape, bf16),
            pltpu.VMEM((n_t, w_out.shape[0], width), bf16),
            pltpu.VMEM(key_cache.shape[1:], bf16),
            pltpu.VMEM(value_cache.shape[1:], bf16),
            pltpu.VMEM((vocab_rows // step, n_dp * capacity, step), bf16),
            pltpu.VMEM((n_part, n_dp, capacity, width // n_part), bf16),
            pltpu.VMEM((n_part, n_dp, capacity, width // n_part), bf16),
            pltpu.VMEM((n_part, n_t, nodes, width // n_part), bf16),
            pltpu.VMEM((nodes, w_query.shape[1]), bf16),
            pltpu.VMEM((n_chip, nodes, width), bf16),
            pltpu.VMEM((n_chip, nodes, width), bf16),
            pltpu.VMEM((n_chip, nodes, width), bf16),
            pltpu.VMEM((n_chip, nodes, width), bf16),
            sems((n_tab,)),
            sems((4,)),
            sems((n_t,)),
            sems((n_dp,)),
            sems((n_dp,)),
            sems((n_part, n_dp)),
            sems((n_part, n_dp)),
            sems((n_part, n_chip)),
            sems((n_part, n_t)),
            sems((n_part, n_chip)),
            sems((n_chip,)),
            sems((n_chip,)),
            sems((n_chip,)),
            sems((n_chip,)),
        ],
        compiler_params=pltpu.CompilerParams(
            collective_id=0, has_side_effects=True, vmem_limit_bytes=62 * 1024 * 1024
        ),
    )(
        tree_ids,
        ancestors,
        lengths,
        gain,
        table,
        w_query,
        w_kv,
        w_out,
        key_cache,
        value_cache,
    ).astype(bf16)


def solution(mesh):
    in_specs = (
        P("dp", None),
        P("dp", None, None),
        P("dp"),
        P("dp", "tensor"),
        P(),
        P(None, "tensor"),
        P(None, None, "tensor"),
        P("tensor", None),
        P("dp", "tensor", None, None),
        P("dp", "tensor", None, None),
    )
    out_specs = P("dp", "tensor")
    return jax.shard_map(shards, mesh=mesh, in_specs=in_specs, out_specs=out_specs, check_vma=False)
```

```python
import functools
import math

import jax
import jax.numpy as jnp
from jax import lax
from jax.experimental import pallas as pl
from jax.experimental.pallas import tpu as pltpu
from jax.sharding import PartitionSpec as P

EPS = 1e-05
NEG = -1e30
THETA = 500000.0
MESH = pl.DeviceIdType.MESH


def layer_kernel(
    n_dp,
    n_t,
    nodes,
    capacity,
    ids_ref,
    anc_ref,
    len_ref,
    gain_ref,
    table_hbm,
    wq_hbm,
    wkv_hbm,
    wout_hbm,
    kc_hbm,
    vc_hbm,
    out_ref,
    ids_all,
    cos_v,
    sin_v,
    table_v,
    wq_v,
    wkv_v,
    wout_v,
    kc_v,
    vc_v,
    acc,
    slot_send,
    slot_recv,
    emb_all,
    ctx_v,
    rs1_send,
    rs1_recv,
    rs2_send,
    rs2_recv,
    table_sem,
    w_sem,
    wout_sem,
    ids_ssem,
    ids_rsem,
    row_ssem,
    row_rsem,
    ag_ssem,
    ag_rsem,
    fw_ssem,
    rs1_ssem,
    rs1_rsem,
    rs2_ssem,
    rs2_rsem,
):
    me = lax.axis_index("dp")
    t = lax.axis_index("tensor")
    chip = t // 2
    parity = t % 2
    partner = t + 1 - 2 * parity
    n_chip = n_t // 2
    vocab_rows, width = table_v.shape
    head_dim = kc_v.shape[-1]
    kv_local = kc_v.shape[0]
    heads = wq_v.shape[1] // head_dim
    groups = heads // kv_local
    slots = n_dp * capacity
    n_part = emb_all.shape[0]
    part_width = width // n_part

    barrier = pltpu.get_barrier_semaphore()
    for k in range(1, n_dp):
        pl.semaphore_signal(
            barrier, inc=1, device_id={"dp": lax.rem(me + k, n_dp)}, device_id_type=MESH
        )
    for k in range(1, n_t):
        pl.semaphore_signal(
            barrier, inc=1, device_id={"tensor": lax.rem(t + k, n_t)}, device_id_type=MESH
        )
    n_tab = table_sem.shape[0]
    tab_step = vocab_rows // n_tab
    table_copies = [
        pltpu.make_async_copy(
            table_hbm.at[pl.ds(i * tab_step, tab_step)],
            table_v.at[pl.ds(i * tab_step, tab_step)],
            table_sem.at[i],
        )
        for i in range(n_tab)
    ]
    for copy in table_copies:
        copy.start()

    pl.semaphore_wait(barrier, n_dp + n_t - 2)

    def dp_copy(src, dst, ssem, rsem, k):
        return pltpu.make_async_remote_copy(
            src_ref=src,
            dst_ref=dst,
            send_sem=ssem,
            recv_sem=rsem,
            device_id={"dp": lax.rem(me + k, n_dp)},
            device_id_type=MESH,
        )

    def t_copy(src, dst, ssem, rsem, target):
        return pltpu.make_async_remote_copy(
            src_ref=src,
            dst_ref=dst,
            send_sem=ssem,
            recv_sem=rsem,
            device_id={"tensor": target},
            device_id_type=MESH,
        )

    ids_copies = [
        dp_copy(ids_ref, ids_all.at[k], ids_ssem.at[k], ids_rsem.at[k], k)
        for k in range(1, n_dp)
    ]
    for copy in ids_copies:
        copy.start()

    sub = lax.broadcasted_iota(jnp.int32, (nodes, nodes), 0)
    lane = lax.broadcasted_iota(jnp.int32, (nodes, nodes), 1)
    earlier = (sub < lane).astype(jnp.float32).astype(jnp.bfloat16)
    slot_index = lax.broadcasted_iota(jnp.int32, (slots, nodes), 0)
    slot_block = slot_index // capacity
    slot_rank = (slot_index - slot_block * capacity).astype(jnp.float32)

    def hits(ids, base):
        mine = (ids >= base) & (ids < base + vocab_rows)
        mine_f = mine.astype(jnp.float32)
        rank = jnp.dot(
            mine_f.astype(jnp.bfloat16), earlier, preferred_element_type=jnp.float32
        )
        return mine & (rank == slot_rank)

    own_ids = jnp.broadcast_to(ids_ref[...], (slots, nodes))
    own_base = lax.rem(me - slot_block + n_dp, n_dp) * vocab_rows
    place = hits(own_ids, own_base).astype(jnp.float32).astype(jnp.bfloat16)

    depth = jnp.sum(anc_ref[0].astype(jnp.float32), axis=1, keepdims=True)
    positions = depth + (len_ref[0] - 1).astype(jnp.float32)
    half_dim = head_dim // 2
    lanes = lax.broadcasted_iota(jnp.int32, (1, head_dim), 1)
    freq_index = jnp.where(lanes < half_dim, lanes, lanes - half_dim).astype(jnp.float32)
    angles = positions * jnp.exp(freq_index * (-2.0 * math.log(THETA) / head_dim))
    cosine = jnp.cos(angles)
    sine = jnp.where(lanes < half_dim, -jnp.sin(angles), jnp.sin(angles))
    cos_v[...] = cosine
    sin_v[...] = sine

    for copy in ids_copies:
        copy.wait_recv()

    w_copies = [
        pltpu.make_async_copy(wq_hbm, wq_v, w_sem.at[0]),
        pltpu.make_async_copy(wkv_hbm, wkv_v, w_sem.at[1]),
        pltpu.make_async_copy(kc_hbm.at[0], kc_v, w_sem.at[2]),
        pltpu.make_async_copy(vc_hbm.at[0], vc_v, w_sem.at[3]),
    ]
    wout_copies = []
    for k in range(n_chip):
        target_chip = lax.rem(chip + k, n_chip)
        for which in range(2):
            chunk = 2 * target_chip + (parity if which else 1 - parity)
            start = pl.multiple_of(chunk * width, width)
            wout_copies.append(
                pltpu.make_async_copy(
                    wout_hbm.at[:, pl.ds(start, width)],
                    wout_v.at[2 * k + which],
                    wout_sem.at[2 * k + which],
                )
            )
    for copy in w_copies + wout_copies:
        copy.start()

    rows_ids = jnp.concatenate(
        [
            jnp.broadcast_to(ids_ref[...] if k == 0 else ids_all[k], (capacity, nodes))
            for k in range(n_dp)
        ],
        axis=0,
    )
    base = me * vocab_rows
    hit = hits(rows_ids, base)
    offset = (
        jnp.sum(
            jnp.where(hit, (rows_ids - base + 1).astype(jnp.float32), 0.0),
            axis=1,
            keepdims=True,
        )
        - 1.0
    ).astype(jnp.int32)
    step = min(8192, vocab_rows)
    step_lane = lax.broadcasted_iota(jnp.int32, (slots, step), 1)
    for copy in table_copies:
        copy.wait()

    acc[...] = jnp.zeros_like(acc)

    def table_step(i, carry):
        first = pl.multiple_of(i * step, step)
        pick = ((step_lane + first) == offset).astype(jnp.float32).astype(jnp.bfloat16)
        acc[...] += jnp.dot(
            pick, table_v[pl.ds(first, step), :], preferred_element_type=jnp.float32
        )
        return carry

    lax.fori_loop(0, vocab_rows // step, table_step, 0)
    row_copies = []
    for q in range(n_part):
        for k in range(n_dp):
            slot_send[q, k] = acc[
                k * capacity : (k + 1) * capacity, q * part_width : (q + 1) * part_width
            ].astype(jnp.bfloat16)
        for k in range(1, n_dp):
            back = n_dp - k
            copy = dp_copy(
                slot_send.at[q, k],
                slot_recv.at[q, back],
                row_ssem.at[q, k],
                row_rsem.at[q, back],
                back,
            )
            copy.start()
            row_copies.append(copy)
        slot_recv[q, 0] = slot_send[q, 0]

    def ag_copy(q, origin, ssem, target):
        return t_copy(
            emb_all.at[q, origin], emb_all.at[q, origin], ssem, ag_rsem.at[q, origin], target
        )

    ag_copies = []
    fw_copies = []

    def forward(q):
        for k in range(1, n_chip):
            origin = lax.rem(t - 2 * k + n_t, n_t)
            copy = ag_copy(q, origin, fw_ssem.at[q, k], partner)
            copy.wait_recv()
            copy.start()
            fw_copies.append(copy)

    for q in range(n_part):
        for k in range(1, n_dp):
            dp_copy(
                slot_send.at[q, k], slot_recv.at[q, k], row_ssem.at[q, k], row_rsem.at[q, k], k
            ).wait_recv()
        arrived = slot_recv[q].reshape(slots, part_width)
        embedded = lax.dot_general(
            place, arrived, (((0,), (0,)), ((), ())), preferred_element_type=jnp.float32
        )
        emb_all[q, t] = embedded.astype(jnp.bfloat16)
        for k in list(range(1, n_chip)) + [0]:
            copy = ag_copy(q, t, ag_ssem.at[q, k], lax.rem(t + 2 * k, n_t) if k else partner)
            copy.start()
            ag_copies.append(copy)
        if q:
            forward(q - 1)
    forward(n_part - 1)
    for q in range(n_part):
        ag_copy(q, partner, ag_ssem.at[q, 0], partner).wait_recv()
        for k in range(1, n_chip):
            origin = lax.rem(partner - 2 * k + n_t, n_t)
            ag_copy(q, origin, ag_ssem.at[q, 0], partner).wait_recv()

    squares = jnp.zeros((nodes, 1), jnp.float32)
    for j in range(n_t):
        for q in range(n_part):
            features = emb_all[q, j].astype(jnp.float32)
            squares = squares + jnp.sum(features * features, axis=1, keepdims=True)
    inv_rms = lax.rsqrt(squares / (n_t * width) + EPS)
    for copy in w_copies:
        copy.wait()
    queries = jnp.zeros((nodes, wq_v.shape[1]), jnp.float32)
    keys_raw = jnp.zeros((nodes, wkv_v.shape[2]), jnp.float32)
    values_raw = jnp.zeros((nodes, wkv_v.shape[2]), jnp.float32)
    for j in range(n_t):
        span = slice(j * width, (j + 1) * width)
        gain = gain_ref[span].astype(jnp.float32)[None, :]
        features = jnp.concatenate([emb_all[q, j] for q in range(n_part)], axis=1)
        normed = (features.astype(jnp.float32) * inv_rms * gain).astype(jnp.bfloat16)
        queries = queries + jnp.dot(normed, wq_v[span, :], preferred_element_type=jnp.float32)
        keys_raw = keys_raw + jnp.dot(normed, wkv_v[0, span, :], preferred_element_type=jnp.float32)
        values_raw = values_raw + jnp.dot(
            normed, wkv_v[1, span, :], preferred_element_type=jnp.float32
        )
    values_new = values_raw.astype(jnp.bfloat16)
    cosine = cos_v[...]
    sine = sin_v[...]

    def rotary(values):
        return (values * cosine + pltpu.roll(values, head_dim // 2, 1) * sine).astype(jnp.bfloat16)

    scale = head_dim ** (-0.5)
    live = lax.broadcasted_iota(jnp.int32, (1, kc_v.shape[1]), 1) < len_ref[0]
    tree = jnp.concatenate([anc_ref[0]] * groups, axis=0) > 0
    contract = (((1,), (1,)), ((), ()))
    for kv in range(kv_local):
        cols = slice(kv * head_dim, (kv + 1) * head_dim)
        query = jnp.concatenate(
            [
                rotary(queries[:, h * head_dim : (h + 1) * head_dim])
                for h in range(kv * groups, (kv + 1) * groups)
            ],
            axis=0,
        )
        key_tree = rotary(keys_raw[:, cols])
        cache_scores = (
            lax.dot_general(query, kc_v[kv], contract, preferred_element_type=jnp.float32) * scale
        )
        cache_scores = jnp.where(live, cache_scores, NEG)
        tree_scores = (
            lax.dot_general(query, key_tree, contract, preferred_element_type=jnp.float32) * scale
        )
        tree_scores = jnp.where(tree, tree_scores, NEG)
        top = jnp.maximum(
            jnp.max(cache_scores, axis=1, keepdims=True),
            jnp.max(tree_scores, axis=1, keepdims=True),
        )
        cache_exp = jnp.exp(cache_scores - top)
        tree_exp = jnp.exp(tree_scores - top)
        denominator = jnp.sum(cache_exp, axis=1, keepdims=True) + jnp.sum(
            tree_exp, axis=1, keepdims=True
        )
        weighted = jnp.dot(
            tree_exp.astype(jnp.bfloat16), values_new[:, cols], preferred_element_type=jnp.float32
        ) + jnp.dot(cache_exp.astype(jnp.bfloat16), vc_v[kv], preferred_element_type=jnp.float32)
        context = (weighted / denominator).astype(jnp.bfloat16)
        for g in range(groups):
            h = kv * groups + g
            ctx_v[:, h * head_dim : (h + 1) * head_dim] = context[g * nodes : (g + 1) * nodes]

    for copy in wout_copies:
        copy.wait()
    contexts = ctx_v[...]
    order = list(range(1, n_chip)) + [0]
    rs1_copies = {}
    for k in order:
        part = jnp.dot(contexts, wout_v[2 * k], preferred_element_type=jnp.float32)
        rs1_send[k] = part.astype(jnp.bfloat16)
        rs1_copies[k] = t_copy(
            rs1_send.at[k], rs1_recv.at[k], rs1_ssem.at[k], rs1_rsem.at[k], partner
        )
        rs1_copies[k].start()
    rs2_copies = []
    total = None
    for k in order:
        part = jnp.dot(contexts, wout_v[2 * k + 1], preferred_element_type=jnp.float32)
        rs1_copies[k].wait_recv()
        both = part + rs1_recv[k].astype(jnp.float32)
        if k:
            rs2_send[k] = both.astype(jnp.bfloat16)
            copy = t_copy(
                rs2_send.at[k], rs2_recv.at[k], rs2_ssem.at[k], rs2_rsem.at[k],
                lax.rem(t + 2 * k, n_t),
            )
            copy.start()
            rs2_copies.append(copy)
        else:
            total = both
    total = total + jnp.concatenate(
        [emb_all[q, t].astype(jnp.float32) for q in range(n_part)], axis=1
    )
    for k, copy in enumerate(rs2_copies):
        copy.wait_recv()
        total = total + rs2_recv[k + 1].astype(jnp.float32)
    out_ref[...] = total
    for copy in (
        ids_copies + row_copies + ag_copies + fw_copies + list(rs1_copies.values()) + rs2_copies
    ):
        copy.wait_send()


def shards(tree_ids, ancestors, lengths, table, gain, w_query, w_kv, w_out, key_cache, value_cache):
    n_dp = lax.axis_size("dp")
    n_t = lax.axis_size("tensor")
    n_chip = n_t // 2
    row_count, nodes = tree_ids.shape
    vocab_rows, width = table.shape
    head_dim = key_cache.shape[3]
    capacity = 2 * ((row_count * nodes + n_dp - 1) // n_dp)
    capacity = 16 * ((capacity + 15) // 16)
    bf16, f32 = jnp.bfloat16, jnp.float32
    n_tab = 4
    n_part = 2
    sems = pltpu.SemaphoreType.DMA
    vmem = pl.BlockSpec(memory_space=pltpu.VMEM)
    hbm = pl.BlockSpec(memory_space=pl.ANY)
    return pl.pallas_call(
        functools.partial(layer_kernel, n_dp, n_t, nodes, capacity),
        out_shape=jax.ShapeDtypeStruct((nodes, width), f32),
        in_specs=[vmem, vmem, pl.BlockSpec(memory_space=pltpu.SMEM), vmem] + [hbm] * 6,
        out_specs=vmem,
        scratch_shapes=[
            pltpu.VMEM((n_dp, 1, nodes), jnp.int32),
            pltpu.VMEM((nodes, head_dim), f32),
            pltpu.VMEM((nodes, head_dim), f32),
            pltpu.VMEM(table.shape, bf16),
            pltpu.VMEM(w_query.shape, bf16),
            pltpu.VMEM(w_kv.shape, bf16),
            pltpu.VMEM((n_t, w_out.shape[0], width), bf16),
            pltpu.VMEM(key_cache.shape[1:], bf16),
            pltpu.VMEM(value_cache.shape[1:], bf16),
            pltpu.VMEM((n_dp * capacity, width), f32),
            pltpu.VMEM((n_part, n_dp, capacity, width // n_part), bf16),
            pltpu.VMEM((n_part, n_dp, capacity, width // n_part), bf16),
            pltpu.VMEM((n_part, n_t, nodes, width // n_part), bf16),
            pltpu.VMEM((nodes, w_query.shape[1]), bf16),
            pltpu.VMEM((n_chip, nodes, width), bf16),
            pltpu.VMEM((n_chip, nodes, width), bf16),
            pltpu.VMEM((n_chip, nodes, width), bf16),
            pltpu.VMEM((n_chip, nodes, width), bf16),
            sems((n_tab,)),
            sems((4,)),
            sems((n_t,)),
            sems((n_dp,)),
            sems((n_dp,)),
            sems((n_part, n_dp)),
            sems((n_part, n_dp)),
            sems((n_part, n_chip)),
            sems((n_part, n_t)),
            sems((n_part, n_chip)),
            sems((n_chip,)),
            sems((n_chip,)),
            sems((n_chip,)),
            sems((n_chip,)),
        ],
        compiler_params=pltpu.CompilerParams(
            collective_id=0, has_side_effects=True, vmem_limit_bytes=62 * 1024 * 1024
        ),
    )(
        tree_ids,
        ancestors,
        lengths,
        gain,
        table,
        w_query,
        w_kv,
        w_out,
        key_cache,
        value_cache,
    ).astype(bf16)


def solution(mesh):
    in_specs = (
        P("dp", None),
        P("dp", None, None),
        P("dp"),
        P("dp", "tensor"),
        P(),
        P(None, "tensor"),
        P(None, None, "tensor"),
        P("tensor", None),
        P("dp", "tensor", None, None),
        P("dp", "tensor", None, None),
    )
    out_specs = P("dp", "tensor")
    return jax.shard_map(shards, mesh=mesh, in_specs=in_specs, out_specs=out_specs, check_vma=False)
```
